128 devices in a mesh: grp: 8 (over z, core), dir: 16 (over x, y).
Axes of the slice: x: 4, y: 4, z: 4, core: 2. Of those that a mesh axis runs over, the one named last changes fastest.
Arguments:
- incident: float32 [4, 1024, 256, 128], P(None, ('grp', 'dir')), may hold values from -6 to 6
- currents_past: bfloat16 [2, 1024, 256, 128], P(None, ('grp', 'dir')), may hold values from -6 to 6
- spectra_past: bfloat16 [2, 128, 1152, 128], P(None, ('grp', 'dir')), may hold values from -9 to 9
- self_inverse: bfloat16 [1024, 256, 256], P(('grp', 'dir')), may hold values from -0.25 to 0.25
- near_blocks: bfloat16 [1024, 6, 2, 256, 256], P(('grp', 'dir')), may hold values from -0.078125 to 0.078125
- neighbours: int32 [1024, 6], P(('grp', 'dir')), may hold values from 0 to 1023, as said below
- near_mask: int32 [1024, 6], P(('grp', 'dir')), may hold values 0 or 1
- ray_out: bfloat16 [256, 1152], replicated, may hold values from -0.375 to 0.375
- ray_in: bfloat16 [1152, 256], replicated, may hold values from -0.1875 to 0.1875
- child_shift: float32 [8, 1152], replicated, may hold values from -1 to 1
- far_sources: int32 [128, 16], replicated, may hold values from 0 to 127
- far_delays: int32 [128, 16], replicated, may hold values from 1 to 2
- translation: float32 [128, 16, 1152], P(None, None, ('grp', 'dir')), may hold values from -0.75 to 0.75
Outputs:
- currents: bfloat16 [4, 1024, 256, 128], P(None, ('grp', 'dir'))
The draws below stay inside these ranges and needn't reach their ends.
Inputs may be any that keep to these rules, and one draw needn't show every extreme that they name: `neighbours`: the entry of group g names a group held by the same device as g, by the device just before it or by the one just after it, devices counted in the order grp then dir, each holding 8 consecutive groups.
All inputs are finite; a program needn't handle non-finite values. No bound on the sum of `near_mask` on one device may be relied on, other than what follows from the above.
Results may differ from the reference program's by a relative error of at most 0.0095.
Values may be sent and summed in bfloat16 or wider, within the bound.
No kernel may reach another device: no remote copies, remote signals or barrier semaphores. Data moves between devices by JAX's collectives and lax.ppermute only.
A program may use at most 128 MiB of HBM per device.

```python
import jax
import jax.numpy as jnp
from jax import lax

E = 256
K = 1152
R = 128
CH = 8
NEAR = 6
LAGS = 2
F = 16
STEPS = 4
G_DEV = 8
GROUPS = 1024
PARENTS = 128


def draw_neighbours(key, part):
    key_device, key_slot = jax.random.split(key)
    owner = jnp.arange(GROUPS, dtype=jnp.int32)[:, None] // G_DEV
    offset = jax.random.randint(key_device, (GROUPS, NEAR), -1, 2)
    device = jnp.clip(owner + offset, 0, GROUPS // G_DEV - 1)
    member = jax.random.randint(key_slot, (GROUPS, NEAR), 0, G_DEV)
    chosen = (device * G_DEV + member).astype(jnp.int32)
    chosen = chosen.at[0, 0].set(0)
    chosen = chosen.at[GROUPS - 1, 0].set(GROUPS - 1)
    return chosen.astype(jnp.int32)


def set_ends(array, rng, least, largest):
    longest = array.shape.index(max(array.shape))
    spots = []
    for shift in (0, 1):
        where = [jax.random.randint(jax.random.fold_in(rng, axis), (), 0, length) for axis, length in enumerate(array.shape)]
        where[longest] = (where[longest] + shift) % array.shape[longest]
        spots.append(tuple(where))
    return array.at[spots[0]].set(least).at[spots[1]].set(largest)


def block_scale(stream_key, dims, cuts, low, top_value):
    level, own = 1.0, jax.random.fold_in(stream_key, 6)
    for dim, blocks in cuts:
        heights = jnp.exp(jax.random.uniform(jax.random.fold_in(own, dim), (blocks,), jnp.float32, low / len(cuts), top_value / len(cuts)))
        level = level * jnp.repeat(heights, dims[dim] // blocks).reshape([-1 if axis == dim else 1 for axis in range(len(dims))])
    return level


def noise(own_key, extent, scale, bound, cuts=(), kind=jnp.bfloat16):
    drawn = jax.random.normal(own_key, extent, jnp.float32) * scale
    if len(cuts) > 0:
        drawn = block_scale(own_key, extent, cuts, -0.22, 0.18) * drawn
    return jnp.clip(drawn, min=-bound, max=bound).astype(kind)


def setup_inputs(seed: int = 0) -> dict:
    keys = jax.random.split(jax.random.key(seed), 14)
    return {
        "incident": noise(keys[0], (STEPS, GROUPS, E, R), 1.0, 6.0, ((1, 128),), jnp.float32),
        "currents_past": noise(keys[1], (LAGS, GROUPS, E, R), 1.0, 6.0, ((1, 128),)),
        "spectra_past": noise(keys[2], (LAGS, PARENTS, K, R), 1.5, 9.0, ((1, 128),)),
        "self_inverse": noise(keys[3], (GROUPS, E, E), (2 * E) ** -0.5, 0.25, ((0, 128),)),
        "near_blocks": noise(keys[4], (GROUPS, NEAR, LAGS, E, E), (2 * NEAR * LAGS * E) ** -0.5, 0.078125, ((0, 128),)),
        "neighbours": draw_neighbours(jax.random.fold_in(keys[13], 71), 0),
        "near_mask": set_ends((jax.random.randint(keys[6], (GROUPS, NEAR), 0, 4) < 3).astype(jnp.int32), jax.random.fold_in(keys[6], 1), 0, 1),
        "ray_out": noise(keys[7], (E, K), E ** -0.5, 0.375),
        "ray_in": noise(keys[8], (K, E), K ** -0.5, 0.1875),
        "child_shift": jnp.clip(jax.random.uniform(keys[9], (CH, K), jnp.float32, -1.0, 1.0), -1.0, 1.0),
        "far_sources": set_ends(jax.random.randint(keys[10], (PARENTS, F), 0, PARENTS), jax.random.fold_in(keys[10], 1), 0, PARENTS - 1).astype(jnp.int32),
        "far_delays": set_ends(jax.random.randint(keys[11], (PARENTS, F), 1, LAGS + 1), jax.random.fold_in(keys[11], 1), 1, LAGS).astype(jnp.int32),
        "translation": noise(keys[12], (PARENTS, F, K), (4 * F) ** -0.5, 0.75, ((2, 128),), jnp.float32),
    }


def near_field(near_blocks, neighbours, near_mask, history):
    def per_group(entries):
        group_blocks, neighbour_ids, live_slots = entries
        picked = jnp.stack([past[neighbour_ids] for past in history], axis=1)
        picked = picked.astype(jnp.float32) * live_slots.astype(jnp.float32)[:, None, None, None]
        return jnp.einsum('nlef,nlfr->er', group_blocks.astype(jnp.float32), picked)
    return lax.map(per_group, (near_blocks, neighbours, near_mask))


def translate(spectra_history, far_sources, far_delays, translation):
    stacked = jnp.stack(spectra_history)

    def per_parent(entries):
        weights, sources, delays = entries
        picked = stacked[delays - 1, sources].astype(jnp.float32)
        return jnp.sum(weights[:, :, None] * picked, axis=0).astype(jnp.bfloat16)
    return lax.map(per_parent, (translation, far_sources, far_delays))


def far_field(incoming, child_shift, ray_in):
    def per_parent(arriving):
        received = (child_shift[:, :, None] * arriving.astype(jnp.float32)).astype(jnp.bfloat16)
        return jnp.einsum('ke,ckr->cer', ray_in.astype(jnp.float32), received.astype(jnp.float32))
    fields = lax.map(per_parent, incoming)
    return fields.reshape(-1, fields.shape[2], fields.shape[3])


def outgoing(current, child_shift, ray_out):
    children = current.reshape(-1, child_shift.shape[0], current.shape[1], current.shape[2])

    def per_parent(members):
        spread = jnp.einsum('ek,cer->ckr', ray_out.astype(jnp.float32), members.astype(jnp.float32))
        return jnp.sum(child_shift[:, :, None] * spread, axis=0).astype(jnp.bfloat16)
    return lax.map(per_parent, children)


def solve(self_inverse, drive):
    def per_group(entries):
        inverse, column = entries
        return jnp.dot(inverse, column, preferred_element_type=jnp.float32).astype(jnp.bfloat16)
    return lax.map(per_group, (self_inverse, drive))


def reference(incident, currents_past, spectra_past, self_inverse, near_blocks, neighbours, near_mask, ray_out, ray_in, child_shift, far_sources, far_delays, translation):
    currents_history = [currents_past[lag_index] for lag_index in range(LAGS)]
    spectra_history = [spectra_past[lag_index] for lag_index in range(LAGS)]
    results = []
    for step_index in range(STEPS):
        near = near_field(near_blocks, neighbours, near_mask, currents_history)
        incoming = translate(spectra_history, far_sources, far_delays, translation)
        far = far_field(incoming, child_shift, ray_in)
        drive = (incident[step_index] - near - far).astype(jnp.bfloat16)
        current = solve(self_inverse, drive)
        results.append(current)
        if step_index + 1 < STEPS:
            spectra_history = [outgoing(current, child_shift, ray_out)] + spectra_history[:-1]
            currents_history = [current] + currents_history[:-1]
    return jnp.stack(results)
```

```python
import functools

import jax
import jax.numpy as jnp
import numpy as np
from jax import lax
from jax.experimental import pallas as pl
from jax.experimental.pallas import tpu as pltpu
from jax.sharding import PartitionSpec as P

LAGS = 2
STEPS = 4
AXES = ("grp", "dir")
CHUNK = 16
BF16 = jnp.bfloat16
F32 = jnp.float32
MIB = 1 << 20


def params(mib, *semantics):
    return pltpu.CompilerParams(
        vmem_limit_bytes=mib * MIB, dimension_semantics=semantics or None
    )


def matmul(left, right):
    return jnp.dot(left, right, preferred_element_type=F32)


def spread_matrix(band, rows):
    out = np.zeros((CHUNK * rows, CHUNK * band), np.float32)
    for b in range(CHUNK):
        for i in range(band):
            out[b * rows + i, b * band + i] = 1.0
    return out


def lagged_spread(band, rows):
    out = np.zeros((LAGS, CHUNK * LAGS * rows, CHUNK * band), np.float32)
    for lag in range(LAGS):
        for b in range(CHUNK):
            for i in range(band):
                out[lag, (b * LAGS + lag) * rows + i, b * band + i] = 1.0
    return out


def pack_kernel(select_ref, past_ref, out_ref):
    tall, wide = select_ref.shape[1], select_ref.shape[2]
    for m in range(past_ref.shape[1] // wide):
        total = matmul(select_ref[0], past_ref[0, pl.ds(m * wide, wide), :])
        for lag in range(1, LAGS):
            total += matmul(select_ref[lag], past_ref[lag, pl.ds(m * wide, wide), :])
        out_ref[pl.ds(m * tall, tall), :] = total.astype(BF16)


def pack(past, band, rows):
    select = jnp.asarray(lagged_spread(band, rows), BF16)
    messages = past.shape[1] // band
    return pl.pallas_call(
        pack_kernel,
        out_shape=jax.ShapeDtypeStruct((messages * LAGS * rows, past.shape[2]), BF16),
        compiler_params=params(16),
        name="pack",
    )(select, past)


def rays_kernel(select_ref, ray_in_ref, ray_out_ref, shift_ref, in_ref, out_ref, shift_out_ref):
    tall, wide = select_ref.shape
    select = select_ref[...]
    outgoing = ray_out_ref[...].astype(F32).T
    shift = shift_ref[...]
    shift = jnp.concatenate([shift, jnp.zeros((128 - shift.shape[0], shift.shape[1]), F32)]).T
    incoming = []
    for m in range(ray_in_ref.shape[0] // wide):
        at, to = m * wide, pl.ds(m * tall, tall)
        incoming.append(matmul(select, ray_in_ref[pl.ds(at, wide), :]))
        out_ref[to, :] = matmul(select, outgoing[at : at + wide, :].astype(BF16)).astype(BF16)
        rest = shift[at : at + wide, :]
        total = jnp.zeros((tall, 128), F32)
        for _ in range(3):
            piece = rest.astype(BF16)
            total += matmul(select, piece)
            rest = rest - piece.astype(F32)
        shift_out_ref[to, :] = total
    in_ref[...] = jnp.concatenate(incoming).T.astype(BF16)


def pad_rays(ray_in, ray_out, child_shift, band, rows):
    select = jnp.asarray(spread_matrix(band, rows), BF16)
    padded = ray_in.shape[0] // band * rows
    return pl.pallas_call(
        rays_kernel,
        out_shape=(
            jax.ShapeDtypeStruct((ray_in.shape[1], padded), BF16),
            jax.ShapeDtypeStruct((padded, ray_out.shape[0]), BF16),
            jax.ShapeDtypeStruct((padded, 128), F32),
        ),
        compiler_params=params(32),
        name="rays",
    )(select, ray_in, ray_out, child_shift)


def weights_kernel(rows, repeat_ref, block_ref, residue_ref, lanes_ref, slots_ref, table_ref, out_ref, wide_ref, keep_ref):
    @pl.when(pl.program_id(0) == 0)
    def _():
        slot = lax.broadcasted_iota(jnp.int32, wide_ref.shape, 0)
        column = lax.broadcasted_iota(jnp.int32, wide_ref.shape, 1)
        offset = column - slot * rows
        inside = jnp.logical_and(offset >= 0, offset < rows)
        wide_ref[...] = jnp.where(inside, 1.0, 0.0).astype(BF16)
        same = residue_ref[...] == lanes_ref[...]
        keep_ref[...] = jnp.where(same, 1.0, 0.0).astype(BF16)

    table = table_ref[...].T.astype(BF16)
    spread = (matmul(repeat_ref[...], table) * block_ref[...]).astype(BF16)
    columns = lax.broadcasted_iota(jnp.int32, (slots_ref.shape[0], wide_ref.shape[0]), 1)
    onehot = jnp.where(slots_ref[...] == columns, 1.0, 0.0).astype(BF16)
    merged = matmul(spread, onehot).astype(BF16)
    out_ref[...] = matmul(merged, wide_ref[...]).astype(BF16) * keep_ref[...]


def far_weights(far_sources, far_delays, translation, rows):
    parents, entries, band = translation.shape
    slots = LAGS * parents
    tall, deep = CHUNK * rows, CHUNK * entries
    slot_index = ((far_delays - 1) * parents + far_sources).reshape(parents * entries, 1)
    table = jnp.pad(translation.reshape(parents * entries, band), ((0, 0), (0, 128 - band)))
    repeat = np.zeros((tall, 128), np.float32)
    repeat[np.arange(tall), np.arange(tall) % rows] = 1.0
    block = (np.arange(tall)[:, None] // rows == np.arange(deep)[None, :] // entries).astype(np.float32)
    residue = (np.arange(tall) % rows).astype(np.int32)[:, None]
    lanes = (np.arange(slots * rows) % rows).astype(np.int32)[None, :]
    whole = lambda i: (0, 0)
    return pl.pallas_call(
        functools.partial(weights_kernel, rows),
        grid=(parents // CHUNK,),
        in_specs=[
            pl.BlockSpec(repeat.shape, whole),
            pl.BlockSpec(block.shape, whole),
            pl.BlockSpec(residue.shape, whole),
            pl.BlockSpec(lanes.shape, whole),
            pl.BlockSpec((deep, 1), lambda i: (i, 0)),
            pl.BlockSpec((deep, 128), lambda i: (i, 0)),
        ],
        out_specs=pl.BlockSpec((tall, slots * rows), lambda i: (i, 0)),
        out_shape=jax.ShapeDtypeStruct((parents * rows, slots * rows), BF16),
        scratch_shapes=[
            pltpu.VMEM((slots, slots * rows), BF16),
            pltpu.VMEM((tall, slots * rows), BF16),
        ],
        compiler_params=params(32, "arbitrary"),
        name="weights",
    )(jnp.asarray(repeat, BF16), jnp.asarray(block), jnp.asarray(residue), jnp.asarray(lanes), slot_index, table)


def translate_kernel(weights_ref, newest_ref, oldest_ref, out_ref):
    depth = newest_ref.shape[0]
    total = matmul(weights_ref[:, :depth], newest_ref[...])
    total += matmul(weights_ref[:, depth:], oldest_ref[...])
    out_ref[...] = total.astype(BF16)


def translate(weights, newest, oldest):
    tall, columns = newest.shape
    tile = 256
    return pl.pallas_call(
        translate_kernel,
        grid=(tall // tile,),
        in_specs=[
            pl.BlockSpec((tile, weights.shape[1]), lambda i: (i, 0)),
            pl.BlockSpec((tall, columns), lambda i: (0, 0)),
            pl.BlockSpec((tall, columns), lambda i: (0, 0)),
        ],
        out_specs=pl.BlockSpec((tile, columns), lambda i: (i, 0)),
        out_shape=jax.ShapeDtypeStruct((tall, columns), BF16),
        compiler_params=params(16, "arbitrary"),
        name="translate",
    )(weights, newest, oldest)


def near_kernel(leads, ids_ref, mask_ref, incident_ref, blocks_ref, *refs):
    sources, (out_ref, window_ref, sems) = refs[: 3 * LAGS], refs[3 * LAGS :]
    groups = out_ref.shape[0] if len(out_ref.shape) == 4 else window_ref.shape[1] // 3
    slots = blocks_ref.shape[1]
    g = pl.program_id(0)

    @pl.when(g == 0)
    def _():
        copies = []
        for lag in range(LAGS):
            for side in range(3):
                source = sources[lag * 3 + side]
                if leads[lag] is not None:
                    source = source.at[leads[lag]]
                copies.append(
                    pltpu.make_async_copy(
                        source, window_ref.at[lag, pl.ds(side * groups, groups)], sems.at[lag * 3 + side]
                    )
                )
        for copy in copies:
            copy.start()
        for copy in copies:
            copy.wait()

    total = incident_ref[0, 0]
    for n in range(slots):
        local = ids_ref[g * slots + n]
        live = mask_ref[g * slots + n] != 0
        for lag in range(LAGS):
            picked = window_ref[lag, local]
            picked = jnp.where(live, picked, jnp.zeros_like(picked))
            total -= matmul(blocks_ref[0, n, lag], picked)
    out_ref[0] = total


def near_field(local_ids, live_slots, incident, step, near_blocks, windows):
    groups, slots, lags, unknowns, _ = near_blocks.shape
    columns = incident.shape[3]
    arrays = [array for parts, _ in windows for array in parts]
    leads = tuple(lead for _, lead in windows)
    return pl.pallas_call(
        functools.partial(near_kernel, leads),
        grid_spec=pltpu.PrefetchScalarGridSpec(
            num_scalar_prefetch=2,
            grid=(groups,),
            in_specs=[
                pl.BlockSpec((1, 1, unknowns, columns), lambda g, ids, mask: (step, g, 0, 0)),
                pl.BlockSpec((1, slots, lags, unknowns, unknowns), lambda g, ids, mask: (g, 0, 0, 0, 0)),
            ]
            + [pl.BlockSpec(memory_space=pl.ANY)] * len(arrays),
            out_specs=pl.BlockSpec((1, unknowns, columns), lambda g, ids, mask: (g, 0, 0)),
            scratch_shapes=[
                pltpu.VMEM((lags, 3 * groups, unknowns, columns), BF16),
                pltpu.SemaphoreType.DMA((3 * lags,)),
            ],
        ),
        out_shape=jax.ShapeDtypeStruct((groups, unknowns, columns), F32),
        compiler_params=params(16, "arbitrary"),
        name="near",
    )(local_ids, live_slots, incident, near_blocks, *arrays)


def solve_kernel(last, aliased, *refs):
    arriving_ref, base_ref, inverse_ref, in_ref, outward_ref, shift_ref = refs[:6]
    outs = refs[7:] if aliased else refs[6:]
    results_ref = outs[0]
    children, unknowns, columns = base_ref.shape
    arriving = arriving_ref[...].astype(F32)
    spectra = None
    for c in range(0, children, 2):
        pair = (c, c + 1)
        received = jnp.concatenate(
            [(shift_ref[:, d : d + 1] * arriving).astype(BF16) for d in pair], axis=1
        )
        fields = matmul(in_ref[...], received)
        currents = []
        for i, d in enumerate(pair):
            drive = (base_ref[d] - fields[:, i * columns : (i + 1) * columns]).astype(BF16)
            current = matmul(inverse_ref[d], drive).astype(BF16)
            results_ref[0, d] = current
            if not last:
                outs[1][d] = current
            currents.append(current)
        if not last:
            spread = matmul(outward_ref[...], jnp.concatenate(currents, axis=1))
            for i, d in enumerate(pair):
                term = shift_ref[:, d : d + 1] * spread[:, i * columns : (i + 1) * columns]
                spectra = term if spectra is None else spectra + term
    if not last:
        outs[2][...] = spectra.astype(BF16)


def solve(step, results, arriving, base, self_inverse, ray_in, ray_out, shift):
    last = step == STEPS - 1
    groups, unknowns, columns = base.shape
    operands = [arriving, base, self_inverse, ray_in, ray_out, shift]
    in_specs = [pl.BlockSpec(a.shape, functools.partial(lambda n, i: (0,) * n, a.ndim)) for a in operands]
    aliases = {}
    if results is not None:
        aliases = {len(operands): 0}
        operands.append(results)
        in_specs.append(pl.BlockSpec(memory_space=pl.ANY))
    out_shape = [jax.ShapeDtypeStruct((STEPS, groups, unknowns, columns), BF16)]
    out_specs = [pl.BlockSpec((1, groups, unknowns, columns), lambda i: (step, 0, 0, 0))]
    if not last:
        out_shape += [
            jax.ShapeDtypeStruct((groups, unknowns, columns), BF16),
            jax.ShapeDtypeStruct(arriving.shape, BF16),
        ]
        out_specs += [
            pl.BlockSpec((groups, unknowns, columns), lambda i: (0, 0, 0)),
            pl.BlockSpec(arriving.shape, lambda i: (0, 0)),
        ]
    return pl.pallas_call(
        functools.partial(solve_kernel, last, results is not None),
        grid=(1,),
        in_specs=in_specs,
        out_specs=out_specs,
        out_shape=out_shape,
        input_output_aliases=aliases,
        compiler_params=params(32, "arbitrary"),
        name="solve",
    )(*operands)


def shifted(block, distance):
    devices = range(lax.axis_size(AXES))
    route = [(i - distance, i) for i in devices if i - distance in devices]
    return lax.ppermute(block, AXES, route)


def window(block):
    return [shifted(block, 1), block, shifted(block, -1)]


def exchange(block, messages):
    tall, columns = block.shape
    cut = block.reshape(messages, tall // messages // 2, 2, columns)
    moved = lax.all_to_all(cut, AXES, split_axis=0, concat_axis=0, tiled=True)
    return moved.reshape(tall, columns)


def exchange_past(past, band, rows):
    packed = pack(past, band, rows)
    columns = packed.shape[1]
    messages = packed.shape[0] // (LAGS * rows)
    cut = packed.reshape(messages, LAGS * rows // 2, 2, columns)
    moved = lax.all_to_all(cut, AXES, split_axis=0, concat_axis=0, tiled=True)
    moved = moved.reshape(messages, LAGS, rows // 2, 2, columns)
    return [moved[:, lag].reshape(messages * rows, columns) for lag in range(LAGS)]


def on_device(
    incident,
    currents_past,
    spectra_past,
    self_inverse,
    near_blocks,
    neighbours,
    near_mask,
    ray_out,
    ray_in,
    child_shift,
    far_sources,
    far_delays,
    translation,
):
    groups = self_inverse.shape[0]
    messages, band = translation.shape[0], translation.shape[2]
    rows = band + band % 2
    first_group = (lax.axis_index(AXES) - 1) * groups
    local_ids = (neighbours - first_group).reshape(-1)
    live_slots = near_mask.reshape(-1)
    bands = exchange_past(spectra_past[:, 0], band, rows)
    past = window(currents_past)
    windows = [(past, 0), (past, 1)]
    rays = pad_rays(ray_in, ray_out, child_shift, band, rows)
    weights = far_weights(far_sources, far_delays, translation, rows)
    results = None
    for step in range(STEPS):
        arriving = exchange(translate(weights, bands[0], bands[1]), messages)
        base = near_field(local_ids, live_slots, incident, step, near_blocks, windows)
        results, *rest = solve(step, results, arriving, base, self_inverse, *rays)
        if rest:
            current, spectra = rest
            windows = [(window(current), None), windows[0]]
            bands = [exchange(spectra, messages), bands[0]]
    return results


def solution(mesh):
    in_specs = (
        P(None, AXES, None, None),
        P(None, AXES, None, None),
        P(None, AXES, None, None),
        P(AXES, None, None),
        P(AXES, None, None, None, None),
        P(AXES, None),
        P(AXES, None),
        P(),
        P(),
        P(),
        P(),
        P(),
        P(None, None, AXES),
    )
    out_specs = P(None, AXES, None, None)
    return jax.shard_map(
        on_device, mesh=mesh, in_specs=in_specs, out_specs=out_specs, check_vma=False
    )
```

```python
import functools

import jax
import jax.numpy as jnp
import numpy as np
from jax import lax
from jax.experimental import pallas as pl
from jax.experimental.pallas import tpu as pltpu
from jax.sharding import PartitionSpec as P

LAGS = 2
STEPS = 4
AXES = ("grp", "dir")
CHUNK = 16
BF16 = jnp.bfloat16
F32 = jnp.float32
HBM = pl.BlockSpec(memory_space=pltpu.HBM)


def params():
    return pltpu.CompilerParams(vmem_limit_bytes=64 << 20)


def matmul(left, right):
    return jnp.dot(left, right, preferred_element_type=F32)


def spread_matrix(band, rows):
    out = np.zeros((CHUNK * rows, CHUNK * band), np.float32)
    for b in range(CHUNK):
        for i in range(band):
            out[b * rows + i, b * band + i] = 1.0
    return out


def lagged_spread(band, rows):
    out = np.zeros((LAGS, CHUNK * LAGS * rows, CHUNK * band), np.float32)
    for lag in range(LAGS):
        for b in range(CHUNK):
            for i in range(band):
                out[lag, (b * LAGS + lag) * rows + i, b * band + i] = 1.0
    return out


def pack_kernel(select_ref, past_ref, out_ref):
    tall, wide = select_ref.shape[1], select_ref.shape[2]
    for m in range(past_ref.shape[1] // wide):
        total = matmul(select_ref[0], past_ref[0, pl.ds(m * wide, wide), :])
        for lag in range(1, LAGS):
            total += matmul(select_ref[lag], past_ref[lag, pl.ds(m * wide, wide), :])
        out_ref[pl.ds(m * tall, tall), :] = total.astype(BF16)


def pack(past, band, rows):
    select = jnp.asarray(lagged_spread(band, rows), BF16)
    messages = past.shape[1] // band
    return pl.pallas_call(
        pack_kernel,
        out_shape=jax.ShapeDtypeStruct((messages * LAGS * rows, past.shape[2]), BF16),
        compiler_params=params(),
        name="pack",
    )(select, past)


def rays_kernel(select_ref, ray_in_ref, ray_out_ref, shift_ref, in_ref, out_ref, shift_out_ref):
    tall, wide = select_ref.shape
    select = select_ref[...]
    outgoing = ray_out_ref[...].astype(F32).T
    shift = shift_ref[...]
    shift = jnp.concatenate([shift, jnp.zeros((128 - shift.shape[0], shift.shape[1]), F32)]).T
    incoming = []
    for m in range(ray_in_ref.shape[0] // wide):
        at, to = m * wide, pl.ds(m * tall, tall)
        incoming.append(matmul(select, ray_in_ref[pl.ds(at, wide), :]))
        out_ref[to, :] = matmul(select, outgoing[at : at + wide, :].astype(BF16)).astype(BF16)
        rest = shift[at : at + wide, :]
        total = jnp.zeros((tall, 128), F32)
        for _ in range(3):
            piece = rest.astype(BF16)
            total += matmul(select, piece)
            rest = rest - piece.astype(F32)
        shift_out_ref[to, :] = total
    in_ref[...] = jnp.concatenate(incoming).T.astype(BF16)


def pad_rays(ray_in, ray_out, child_shift, band, rows):
    select = jnp.asarray(spread_matrix(band, rows), BF16)
    padded = ray_in.shape[0] // band * rows
    return pl.pallas_call(
        rays_kernel,
        out_shape=(
            jax.ShapeDtypeStruct((ray_in.shape[1], padded), BF16),
            jax.ShapeDtypeStruct((padded, ray_out.shape[0]), BF16),
            jax.ShapeDtypeStruct((padded, 128), F32),
        ),
        compiler_params=params(),
        name="rays",
    )(select, ray_in, ray_out, child_shift)


def weights_kernel(sources_ref, delays_ref, table_ref, out_ref):
    band, entries, parents = table_ref.shape
    slots = LAGS * parents
    slot = lax.broadcasted_iota(jnp.int32, (slots, parents), 0)
    wanted = (delays_ref[...] - 1) * parents + sources_ref[...]
    for k in range(band):
        total = jnp.zeros((slots, parents), F32)
        for f in range(entries):
            total += jnp.where(slot == wanted[f : f + 1, :], table_ref[k, f : f + 1, :], 0.0)
        out_ref[k] = total.T.astype(BF16)


def far_weights(far_sources, far_delays, translation):
    parents, _, band = translation.shape
    return pl.pallas_call(
        weights_kernel,
        out_shape=jax.ShapeDtypeStruct((band, parents, LAGS * parents), BF16),
        compiler_params=params(),
        name="weights",
    )(far_sources.T, far_delays.T, jnp.transpose(translation, (2, 1, 0)))


def translate_kernel(rows, places, weights_ref, *refs):
    inputs, out_ref, wide, result_ref = refs[:-4], refs[-4], refs[-3:-1], refs[-1]
    band, parents, _ = weights_ref.shape
    for source, scratch in zip(inputs, wide):
        scratch[: source.shape[0], :] = source[...].astype(F32)
    result_ref[...] = jnp.zeros_like(result_ref)
    for k in range(band):
        picked = [
            wide[array][pl.ds(start + k, parents, stride=stride), :].astype(BF16)
            for array, start, stride in places
        ]
        total = matmul(weights_ref[k], jnp.concatenate(picked, axis=0))
        result_ref[pl.ds(k, parents, stride=rows), :] = total
    out_ref[...] = result_ref[...].astype(BF16)


def translate(weights, rows, newest, oldest):
    _, parents, _ = weights.shape
    arrays, places = [], []
    for array, start, stride in (newest, oldest):
        known = [i for i, other in enumerate(arrays) if other is array]
        if not known:
            arrays.append(array)
        places.append((known[0] if known else len(arrays) - 1, start, stride))
    columns = newest[0].shape[1]
    longest = max(array.shape[0] for array in arrays)
    return pl.pallas_call(
        functools.partial(translate_kernel, rows, tuple(places)),
        out_shape=jax.ShapeDtypeStruct((parents * rows, columns), BF16),
        scratch_shapes=[
            pltpu.VMEM((longest, columns), F32),
            pltpu.VMEM((longest, columns), F32),
            pltpu.VMEM((parents * rows, columns), F32),
        ],
        compiler_params=params(),
        name="translate",
    )(weights, *arrays)


def near_kernel(step, leads, first_ref, ids_ref, mask_ref, incident_ref, blocks_ref, *refs):
    sources, refs = refs[: 3 * LAGS], refs[3 * LAGS :]
    out_ref, window_ref, matrices_ref, field_ref, window_sems, block_sems, field_sem = refs
    groups, slots = matrices_ref.shape[:2]
    moves = []
    for lag in range(LAGS):
        for side in range(3):
            source = sources[lag * 3 + side]
            if leads[lag] is not None:
                source = source.at[leads[lag]]
            target = window_ref.at[lag, pl.ds(side * groups, groups)]
            moves.append(pltpu.make_async_copy(source, target, window_sems.at[lag * 3 + side]))
    moves.append(pltpu.make_async_copy(incident_ref.at[step], field_ref, field_sem))
    blocks = [
        pltpu.make_async_copy(blocks_ref.at[g], matrices_ref.at[g], block_sems.at[g])
        for g in range(groups)
    ]
    for move in moves + blocks:
        move.start()
    dead = window_ref.shape[1] - 1
    for lag in range(LAGS):
        window_ref[lag, dead] = jnp.zeros(window_ref.shape[2:], window_ref.dtype)
    for move in moves:
        move.wait()
    for g in range(groups):
        blocks[g].wait()
        total = field_ref[g]
        for n in range(slots):
            picked = jnp.where(mask_ref[g, n] != 0, ids_ref[g, n] - first_ref[0], dead)
            for lag in range(LAGS):
                total -= matmul(matrices_ref[g, n, lag], window_ref[lag, picked])
        out_ref[g] = total


def near_field(places, incident, step, near_blocks, windows):
    groups, _, lags, unknowns, _ = near_blocks.shape
    columns = incident.shape[3]
    arrays = [array for parts, _ in windows for array in parts]
    leads = tuple(lead for _, lead in windows)
    return pl.pallas_call(
        functools.partial(near_kernel, step, leads),
        in_specs=[pl.BlockSpec(memory_space=pltpu.SMEM)] * 3 + [HBM] * (2 + len(arrays)),
        out_shape=jax.ShapeDtypeStruct((groups, unknowns, columns), F32),
        scratch_shapes=[
            pltpu.VMEM((lags, 3 * groups + 1, unknowns, columns), BF16),
            pltpu.VMEM(near_blocks.shape, BF16),
            pltpu.VMEM((groups, unknowns, columns), F32),
            pltpu.SemaphoreType.DMA((3 * lags,)),
            pltpu.SemaphoreType.DMA((groups,)),
            pltpu.SemaphoreType.DMA,
        ],
        compiler_params=params(),
        name="near",
    )(*places, incident, near_blocks, *arrays)


def solve_kernel(step, aliased, *refs):
    last = step == STEPS - 1
    inputs = refs[:6]
    count = 1 if last else 3
    outs = refs[6 + aliased : 6 + aliased + count]
    scratch = refs[6 + aliased + count :]
    buffers, (currents_ref, spectra_ref, in_sems, out_sems) = scratch[:6], scratch[6:]
    loads = [
        pltpu.make_async_copy(source, buffer, in_sems.at[i])
        for i, (source, buffer) in enumerate(zip(inputs, buffers))
        if not (last and i == 5)
    ]
    for load in loads:
        load.start()
    arriving_ref, in_ref, shift_ref, base_ref, inverse_ref, outward_ref = buffers
    children, _, columns = base_ref.shape
    pairs = [(c, c + 1) for c in range(0, children, 2)]
    stores = []

    def store(source, target):
        stores.append(pltpu.make_async_copy(source, target, out_sems.at[len(stores)]))
        stores[-1].start()

    for i in range(3):
        loads[i].wait()
    arriving = arriving_ref[...].astype(F32)
    fields = []
    for pair in pairs:
        received = jnp.concatenate(
            [(shift_ref[:, d : d + 1] * arriving).astype(BF16) for d in pair], axis=1
        )
        fields.append(matmul(in_ref[...], received))
    for i in range(3, 5):
        loads[i].wait()
    for pair, field in zip(pairs, fields):
        for i, d in enumerate(pair):
            drive = (base_ref[d] - field[:, i * columns : (i + 1) * columns]).astype(BF16)
            currents_ref[d] = matmul(inverse_ref[d], drive).astype(BF16)
    store(currents_ref, outs[0].at[step])
    if not last:
        store(currents_ref, outs[1])
        loads[5].wait()
        spectra = None
        for pair in pairs:
            spread = matmul(
                outward_ref[...], jnp.concatenate([currents_ref[d] for d in pair], axis=1)
            )
            for i, d in enumerate(pair):
                term = shift_ref[:, d : d + 1] * spread[:, i * columns : (i + 1) * columns]
                spectra = term if spectra is None else spectra + term
        spectra_ref[...] = spectra.astype(BF16)
        store(spectra_ref, outs[2])
    for copy in stores:
        copy.wait()


def solve(step, results, arriving, base, self_inverse, ray_in, ray_out, shift):
    last = step == STEPS - 1
    groups, unknowns, columns = base.shape
    operands = [arriving, ray_in, shift, base, self_inverse, ray_out]
    buffers = [pltpu.VMEM(a.shape, a.dtype) for a in operands]
    aliased = results is not None
    out_shape = [jax.ShapeDtypeStruct((STEPS, groups, unknowns, columns), BF16)]
    if not last:
        out_shape += [
            jax.ShapeDtypeStruct((groups, unknowns, columns), BF16),
            jax.ShapeDtypeStruct(arriving.shape, BF16),
        ]
    if aliased:
        operands.append(results)
    return pl.pallas_call(
        functools.partial(solve_kernel, step, aliased),
        in_specs=[HBM] * len(operands),
        out_specs=[HBM] * len(out_shape),
        out_shape=out_shape,
        input_output_aliases={len(operands) - 1: 0} if aliased else {},
        scratch_shapes=buffers
        + [
            pltpu.VMEM((groups, unknowns, columns), BF16),
            pltpu.VMEM(arriving.shape, BF16),
            pltpu.SemaphoreType.DMA((6,)),
            pltpu.SemaphoreType.DMA((3,)),
        ],
        compiler_params=params(),
        name="solve",
    )(*operands)


def shifted(block, distance):
    devices = range(lax.axis_size(AXES))
    route = [(i - distance, i) for i in devices if i - distance in devices]
    return lax.ppermute(block, AXES, route)


def window(block):
    return [shifted(block, 1), block, shifted(block, -1)]


def exchange(block, messages):
    tall, columns = block.shape
    cut = block.reshape(messages, tall // messages // 2, 2, columns)
    moved = lax.all_to_all(cut, AXES, split_axis=0, concat_axis=0, tiled=True)
    return moved.reshape(tall, columns)


def on_device(
    incident,
    currents_past,
    spectra_past,
    self_inverse,
    near_blocks,
    neighbours,
    near_mask,
    ray_out,
    ray_in,
    child_shift,
    far_sources,
    far_delays,
    translation,
):
    groups = self_inverse.shape[0]
    messages, band = translation.shape[0], translation.shape[2]
    rows = band + band % 2
    first_group = (lax.axis_index(AXES) - 1) * groups
    places = (first_group.reshape(1), neighbours, near_mask)
    packed = pack(spectra_past[:, 0], band, rows)
    opening = exchange(packed, messages)
    past = window(currents_past)
    bands = [(opening, lag * rows, LAGS * rows) for lag in range(LAGS)]
    windows = [(past, 0), (past, 1)]
    rays = pad_rays(ray_in, ray_out, child_shift, band, rows)
    weights = far_weights(far_sources, far_delays, translation)
    weights, rays = lax.optimization_barrier((weights, rays))
    results = None
    for step in range(STEPS):
        arriving = exchange(translate(weights, rows, *bands), messages)
        base = near_field(places, incident, step, near_blocks, windows)
        results, *rest = solve(step, results, arriving, base, self_inverse, *rays)
        if rest:
            current, spectra = rest
            windows = [(window(current), None), windows[0]]
            bands = [(exchange(spectra, messages), 0, rows), bands[0]]
    return results


def solution(mesh):
    in_specs = (
        P(None, AXES, None, None),
        P(None, AXES, None, None),
        P(None, AXES, None, None),
        P(AXES, None, None),
        P(AXES, None, None, None, None),
        P(AXES, None),
        P(AXES, None),
        P(),
        P(),
        P(),
        P(),
        P(),
        P(None, None, AXES),
    )
    out_specs = P(None, AXES, None, None)
    return jax.shard_map(
        on_device, mesh=mesh, in_specs=in_specs, out_specs=out_specs, check_vma=False
    )
```

```python
import functools

import jax
import jax.numpy as jnp
import numpy as np
from jax import lax
from jax.experimental import pallas as pl
from jax.experimental.pallas import tpu as pltpu
from jax.sharding import PartitionSpec as P

LAGS = 2
STEPS = 4
AXES = ("grp", "dir")
CHUNK = 16
UNIT = 2
BF16 = jnp.bfloat16
F32 = jnp.float32
HBM = pl.BlockSpec(memory_space=pltpu.HBM)


def params():
    return pltpu.CompilerParams(vmem_limit_bytes=64 << 20)


def matmul(left, right):
    return jnp.dot(left, right, preferred_element_type=F32)


def spread_matrix(band, rows):
    out = np.zeros((CHUNK * rows, CHUNK * band), np.float32)
    for b in range(CHUNK):
        for i in range(band):
            out[b * rows + i, b * band + i] = 1.0
    return out


def lagged_spread(band, rows):
    out = np.zeros((LAGS, CHUNK * LAGS * rows, CHUNK * band), np.float32)
    for lag in range(LAGS):
        for b in range(CHUNK):
            for i in range(band):
                out[lag, (b * LAGS + lag) * rows + i, b * band + i] = 1.0
    return out


def pack_kernel(select_ref, past_ref, out_ref):
    tall, wide = select_ref.shape[1], select_ref.shape[2]
    for m in range(past_ref.shape[1] // wide):
        total = matmul(select_ref[0], past_ref[0, pl.ds(m * wide, wide), :])
        for lag in range(1, LAGS):
            total += matmul(select_ref[lag], past_ref[lag, pl.ds(m * wide, wide), :])
        out_ref[pl.ds(m * tall, tall), :] = total.astype(BF16)


def pack(past, band, rows):
    select = jnp.asarray(lagged_spread(band, rows), BF16)
    messages = past.shape[1] // band
    return pl.pallas_call(
        pack_kernel,
        out_shape=jax.ShapeDtypeStruct((messages * LAGS * rows, past.shape[2]), BF16),
        compiler_params=params(),
        name="pack",
    )(select, past)


def rays_kernel(select_ref, ray_in_ref, ray_out_ref, shift_ref, in_ref, out_ref, shift_out_ref):
    tall, wide = select_ref.shape
    select = select_ref[...]
    outgoing = ray_out_ref[...].astype(F32).T
    shift = shift_ref[...]
    shift = jnp.concatenate([shift, jnp.zeros((128 - shift.shape[0], shift.shape[1]), F32)]).T
    incoming = []
    for m in range(ray_in_ref.shape[0] // wide):
        at, to = m * wide, pl.ds(m * tall, tall)
        incoming.append(matmul(select, ray_in_ref[pl.ds(at, wide), :]))
        out_ref[to, :] = matmul(select, outgoing[at : at + wide, :].astype(BF16)).astype(BF16)
        shift_out_ref[to, :] = matmul(select, shift[at : at + wide, :].astype(BF16)).astype(BF16)
    in_ref[...] = jnp.concatenate(incoming).T.astype(BF16)


def pad_rays(ray_in, ray_out, child_shift, band, rows):
    select = jnp.asarray(spread_matrix(band, rows), BF16)
    padded = ray_in.shape[0] // band * rows
    return pl.pallas_call(
        rays_kernel,
        out_shape=(
            jax.ShapeDtypeStruct((ray_in.shape[1], padded), BF16),
            jax.ShapeDtypeStruct((padded, ray_out.shape[0]), BF16),
            jax.ShapeDtypeStruct((padded, 128), BF16),
        ),
        compiler_params=params(),
        name="rays",
    )(select, ray_in, ray_out, child_shift)


def weights_kernel(sources_ref, delays_ref, table_ref, out_ref):
    band, entries, parents = table_ref.shape
    slots = LAGS * parents
    slot = lax.broadcasted_iota(jnp.int32, (slots, parents), 0)
    wanted = (delays_ref[...] - 1) * parents + sources_ref[...]
    for k in range(band):
        total = jnp.zeros((slots, parents), F32)
        for f in range(entries):
            total += jnp.where(slot == wanted[f : f + 1, :], table_ref[k, f : f + 1, :], 0.0)
        out_ref[k] = total.T.astype(BF16)


def far_weights(far_sources, far_delays, translation):
    parents, _, band = translation.shape
    return pl.pallas_call(
        weights_kernel,
        out_shape=jax.ShapeDtypeStruct((band, parents, LAGS * parents), BF16),
        compiler_params=params(),
        name="weights",
    )(far_sources.T, far_delays.T, jnp.transpose(translation, (2, 1, 0)))


def translate_kernel(rows, places, weights_ref, *refs):
    inputs, out_ref, wide, result_ref = refs[:-4], refs[-4], refs[-3:-1], refs[-1]
    band, parents, _ = weights_ref.shape
    for source, scratch in zip(inputs, wide):
        scratch[: source.shape[0], :] = source[...].astype(F32)
    result_ref[...] = jnp.zeros_like(result_ref)
    for k in range(band):
        picked = [
            wide[array][pl.ds(start + k, parents, stride=stride), :].astype(BF16)
            for array, start, stride in places
        ]
        total = matmul(weights_ref[k], jnp.concatenate(picked, axis=0))
        result_ref[pl.ds(k, parents, stride=rows), :] = total
    out_ref[...] = result_ref[...].astype(BF16)


def translate(weights, rows, newest, oldest):
    _, parents, _ = weights.shape
    arrays, places = [], []
    for array, start, stride in (newest, oldest):
        known = [i for i, other in enumerate(arrays) if other is array]
        if not known:
            arrays.append(array)
        places.append((known[0] if known else len(arrays) - 1, start, stride))
    columns = newest[0].shape[1]
    longest = max(array.shape[0] for array in arrays)
    return pl.pallas_call(
        functools.partial(translate_kernel, rows, tuple(places)),
        out_shape=jax.ShapeDtypeStruct((parents * rows, columns), BF16),
        scratch_shapes=[
            pltpu.VMEM((longest, columns), F32),
            pltpu.VMEM((longest, columns), F32),
            pltpu.VMEM((parents * rows, columns), F32),
        ],
        compiler_params=params(),
        name="translate",
    )(weights, *arrays)


def near_kernel(step, leads, first_ref, ids_ref, mask_ref, incident_ref, blocks_ref, *refs):
    sources, refs = refs[: 3 * LAGS], refs[3 * LAGS :]
    out_ref, window_ref, matrices_ref, field_ref, sems, block_sems, out_sems = refs
    groups, slots = matrices_ref.shape[:2]
    parts = groups // UNIT
    dead = window_ref.shape[1] - 1

    def load(i):
        chosen = pl.ds(i * UNIT, UNIT)
        return pltpu.make_async_copy(blocks_ref.at[chosen], matrices_ref.at[chosen], block_sems.at[i])

    def save(i):
        chosen = pl.ds(i * UNIT, UNIT)
        return pltpu.make_async_copy(field_ref.at[chosen], out_ref.at[chosen], out_sems.at[i])

    moves = [pltpu.make_async_copy(incident_ref.at[step], field_ref, sems.at[0])]
    for index, lead in enumerate(leads):
        for side in range(3):
            source = sources[index * 3 + side]
            target = window_ref.at[index, pl.ds(side * groups, groups)]
            moves.append(
                pltpu.make_async_copy(
                    source if lead is None else source.at[lead], target, sems.at[index * 3 + side + 1]
                )
            )
    for move in moves:
        move.start()
    for i in range(2):
        load(i).start()
    for index in range(LAGS):
        window_ref[index, dead] = jnp.zeros(window_ref.shape[2:], window_ref.dtype)
    for move in moves:
        move.wait()

    def body(i, carry):
        load(i).wait()

        @pl.when(i + 2 < parts)
        def _():
            load(i + 2).start()

        for j in range(UNIT):
            g = i * UNIT + j
            total = field_ref[g]
            for n in range(slots):
                picked = jnp.where(mask_ref[g, n] != 0, ids_ref[g, n] - first_ref[0], dead)
                for index in range(LAGS):
                    total -= matmul(matrices_ref[g, n, index], window_ref[index, picked])
            field_ref[g] = total
        save(i).start()
        return carry

    lax.fori_loop(0, parts, body, 0)
    for i in range(parts):
        save(i).wait()


def near_field(places, incident, step, near_blocks, windows):
    groups, slots, _, unknowns, _ = near_blocks.shape
    columns = incident.shape[-1]
    arrays = [array for parts, _ in windows for array in parts]
    leads = tuple(lead for _, lead in windows)
    return pl.pallas_call(
        functools.partial(near_kernel, step, leads),
        in_specs=[pl.BlockSpec(memory_space=pltpu.SMEM)] * 3 + [HBM] * (2 + len(arrays)),
        out_specs=HBM,
        out_shape=jax.ShapeDtypeStruct((groups, unknowns, columns), F32),
        scratch_shapes=[
            pltpu.VMEM((LAGS, 3 * groups + 1, unknowns, columns), BF16),
            pltpu.VMEM((groups, slots, LAGS, unknowns, unknowns), BF16),
            pltpu.VMEM((groups, unknowns, columns), F32),
            pltpu.SemaphoreType.DMA((3 * LAGS + 1,)),
            pltpu.SemaphoreType.DMA((groups // UNIT,)),
            pltpu.SemaphoreType.DMA((groups // UNIT,)),
        ],
        compiler_params=params(),
        name="near",
    )(*places, incident, near_blocks, *arrays)


def solve_kernel(step, aliased, *refs):
    last = step == STEPS - 1
    inputs = refs[:6]
    count = 1 if last else 3
    outs = refs[6 + aliased : 6 + aliased + count]
    scratch = refs[6 + aliased + count :]
    buffers, (currents_ref, spectra_ref, in_sems, out_sems) = scratch[:6], scratch[6:]
    loads = [
        pltpu.make_async_copy(source, buffer, in_sems.at[i])
        for i, (source, buffer) in enumerate(zip(inputs, buffers))
        if not (last and i == 5)
    ]
    for load in loads:
        load.start()
    arriving_ref, in_ref, shift_ref, base_ref, inverse_ref, outward_ref = buffers
    children, _, columns = base_ref.shape
    pairs = [(c, c + 1) for c in range(0, children, 2)]
    stores = []

    def store(source, target):
        stores.append(pltpu.make_async_copy(source, target, out_sems.at[len(stores)]))
        stores[-1].start()

    for i in range(3):
        loads[i].wait()
    arriving = arriving_ref[...]
    fields = []
    for pair in pairs:
        received = jnp.concatenate(
            [shift_ref[:, d : d + 1] * arriving for d in pair], axis=1
        )
        fields.append(matmul(in_ref[...], received))
    for i in range(3, 5):
        loads[i].wait()
    for pair, field in zip(pairs, fields):
        for i, d in enumerate(pair):
            drive = (base_ref[d] - field[:, i * columns : (i + 1) * columns]).astype(BF16)
            currents_ref[d] = matmul(inverse_ref[d], drive).astype(BF16)
    store(currents_ref, outs[0].at[step])
    if not last:
        store(currents_ref, outs[1])
        loads[5].wait()
        spectra = None
        for pair in pairs:
            spread = matmul(
                outward_ref[...], jnp.concatenate([currents_ref[d] for d in pair], axis=1)
            )
            for i, d in enumerate(pair):
                term = shift_ref[:, d : d + 1].astype(F32) * spread[:, i * columns : (i + 1) * columns]
                spectra = term if spectra is None else spectra + term
        spectra_ref[...] = spectra.astype(BF16)
        store(spectra_ref, outs[2])
    for copy in stores:
        copy.wait()


def solve(step, results, arriving, base, self_inverse, ray_in, ray_out, shift):
    last = step == STEPS - 1
    groups, unknowns, columns = base.shape
    operands = [arriving, ray_in, shift, base, self_inverse, ray_out]
    buffers = [pltpu.VMEM(a.shape, a.dtype) for a in operands]
    aliased = results is not None
    out_shape = [jax.ShapeDtypeStruct((STEPS, groups, unknowns, columns), BF16)]
    if not last:
        out_shape += [
            jax.ShapeDtypeStruct((groups, unknowns, columns), BF16),
            jax.ShapeDtypeStruct(arriving.shape, BF16),
        ]
    if aliased:
        operands.append(results)
    return pl.pallas_call(
        functools.partial(solve_kernel, step, aliased),
        in_specs=[HBM] * len(operands),
        out_specs=[HBM] * len(out_shape),
        out_shape=out_shape,
        input_output_aliases={len(operands) - 1: 0} if aliased else {},
        scratch_shapes=buffers
        + [
            pltpu.VMEM((groups, unknowns, columns), BF16),
            pltpu.VMEM(arriving.shape, BF16),
            pltpu.SemaphoreType.DMA((6,)),
            pltpu.SemaphoreType.DMA((3,)),
        ],
        compiler_params=params(),
        name="solve",
    )(*operands)


def shifted(block, distance):
    devices = range(lax.axis_size(AXES))
    route = [(i - distance, i) for i in devices if i - distance in devices]
    return lax.ppermute(block, AXES, route)


def window(block):
    return [shifted(block, 1), block, shifted(block, -1)]


def exchange(block, messages):
    tall, columns = block.shape
    cut = block.reshape(messages, tall // messages // 2, 2, columns)
    moved = lax.all_to_all(cut, AXES, split_axis=0, concat_axis=0, tiled=True)
    return moved.reshape(tall, columns)


def on_device(
    incident,
    currents_past,
    spectra_past,
    self_inverse,
    near_blocks,
    neighbours,
    near_mask,
    ray_out,
    ray_in,
    child_shift,
    far_sources,
    far_delays,
    translation,
):
    groups = self_inverse.shape[0]
    messages, band = translation.shape[0], translation.shape[2]
    rows = band + band % 2
    first_group = (lax.axis_index(AXES) - 1) * groups
    places = (first_group.reshape(1), neighbours, near_mask)
    packed = pack(spectra_past[:, 0], band, rows)
    opening = exchange(packed, messages)
    past = window(currents_past)
    bands = [(opening, lag * rows, LAGS * rows) for lag in range(LAGS)]
    windows = [(past, 0), (past, 1)]
    rays = pad_rays(ray_in, ray_out, child_shift, band, rows)
    weights = far_weights(far_sources, far_delays, translation)
    weights, rays = lax.optimization_barrier((weights, rays))
    results = None
    for step in range(STEPS):
        arriving = exchange(translate(weights, rows, *bands), messages)
        base = near_field(places, incident, step, near_blocks, windows)
        results, *rest = solve(step, results, arriving, base, self_inverse, *rays)
        if rest:
            current, spectra = rest
            moved = exchange(spectra, messages)
            nearby = window(current)
            windows = [(nearby, None), windows[0]]
            bands = [(moved, 0, rows), bands[0]]
    return results


def solution(mesh):
    in_specs = (
        P(None, AXES, None, None),
        P(None, AXES, None, None),
        P(None, AXES, None, None),
        P(AXES, None, None),
        P(AXES, None, None, None, None),
        P(AXES, None),
        P(AXES, None),
        P(),
        P(),
        P(),
        P(),
        P(),
        P(None, None, AXES),
    )
    out_specs = P(None, AXES, None, None)
    return jax.shard_map(
        on_device, mesh=mesh, in_specs=in_specs, out_specs=out_specs, check_vma=False
    )
```

```python
import functools

import jax
import jax.numpy as jnp
import numpy as np
from jax import lax
from jax.experimental import pallas as pl
from jax.experimental.pallas import tpu as pltpu
from jax.sharding import PartitionSpec as P

LAGS = 2
STEPS = 4
AXES = ("grp", "dir")
CHUNK = 16
UNIT = 1
PIECES = 4
BF16 = jnp.bfloat16
F32 = jnp.float32
HBM = pl.BlockSpec(memory_space=pltpu.HBM)


def params():
    return pltpu.CompilerParams(vmem_limit_bytes=64 << 20)


def matmul(left, right):
    return jnp.dot(left, right, preferred_element_type=F32)


def spread_matrix(band, rows):
    out = np.zeros((CHUNK * rows, CHUNK * band), np.float32)
    for b in range(CHUNK):
        for i in range(band):
            out[b * rows + i, b * band + i] = 1.0
    return out


def pack_kernel(rows, past_ref, out_ref, taken_ref, wide_ref, result_ref, rounded_ref, in_sems, out_sems):
    lags, directions, columns = past_ref.shape
    parents = out_ref.shape[0] // (lags * rows)
    band = directions // parents
    part = out_ref.shape[0] // PIECES
    loads = [
        pltpu.make_async_copy(past_ref.at[lag], taken_ref.at[lag], in_sems.at[lag]) for lag in range(lags)
    ]
    for load in loads:
        load.start()
    for lag in range(lags):
        for k in range(band, rows):
            result_ref[pl.ds(lag * rows + k, parents, stride=lags * rows), :] = jnp.zeros((parents, columns), F32)
        loads[lag].wait()
        wide_ref[lag] = taken_ref[lag].astype(F32)
        for k in range(band):
            result_ref[pl.ds(lag * rows + k, parents, stride=lags * rows), :] = wide_ref[
                lag, pl.ds(k, parents, stride=band), :
            ]
    stores = []
    for piece in range(PIECES):
        chosen = pl.ds(piece * part, part)
        rounded_ref[chosen, :] = result_ref[chosen, :].astype(BF16)
        stores.append(pltpu.make_async_copy(rounded_ref.at[chosen], out_ref.at[chosen], out_sems.at[piece]))
        stores[-1].start()
    for store in stores:
        store.wait()


def pack(past, band, rows):
    lags, directions, columns = past.shape
    tall = directions // band * lags * rows
    return pl.pallas_call(
        functools.partial(pack_kernel, rows),
        in_specs=[HBM],
        out_specs=HBM,
        out_shape=jax.ShapeDtypeStruct((tall, columns), BF16),
        scratch_shapes=[
            pltpu.VMEM(past.shape, BF16),
            pltpu.VMEM(past.shape, F32),
            pltpu.VMEM((tall, columns), F32),
            pltpu.VMEM((tall, columns), BF16),
            pltpu.SemaphoreType.DMA((lags,)),
            pltpu.SemaphoreType.DMA((PIECES,)),
        ],
        compiler_params=params(),
        name="pack",
    )(past)


def rays_kernel(select_ref, ray_in_ref, ray_out_ref, shift_ref, in_ref, out_ref, shift_out_ref):
    tall, wide = select_ref.shape
    select = select_ref[...]
    outgoing = ray_out_ref[...].astype(F32).T
    shift = shift_ref[...]
    shift = jnp.concatenate([shift, jnp.zeros((128 - shift.shape[0], shift.shape[1]), F32)]).T
    incoming = []
    for m in range(ray_in_ref.shape[0] // wide):
        at, to = m * wide, pl.ds(m * tall, tall)
        incoming.append(matmul(select, ray_in_ref[pl.ds(at, wide), :]))
        out_ref[to, :] = matmul(select, outgoing[at : at + wide, :].astype(BF16)).astype(BF16)
        shift_out_ref[to, :] = matmul(select, shift[at : at + wide, :].astype(BF16)).astype(BF16)
    in_ref[...] = jnp.concatenate(incoming).T.astype(BF16)


def pad_rays(ray_in, ray_out, child_shift, band, rows):
    select = jnp.asarray(spread_matrix(band, rows), BF16)
    padded = ray_in.shape[0] // band * rows
    return pl.pallas_call(
        rays_kernel,
        out_shape=(
            jax.ShapeDtypeStruct((ray_in.shape[1], padded), BF16),
            jax.ShapeDtypeStruct((padded, ray_out.shape[0]), BF16),
            jax.ShapeDtypeStruct((padded, 128), BF16),
        ),
        compiler_params=params(),
        name="rays",
    )(select, ray_in, ray_out, child_shift)


def weights_kernel(sources_ref, delays_ref, table_ref, out_ref):
    band, entries, parents = table_ref.shape
    slots = LAGS * parents
    slot = lax.broadcasted_iota(jnp.int32, (slots, parents), 0)
    wanted = (delays_ref[...] - 1) * parents + sources_ref[...]
    for k in range(band):
        total = jnp.zeros((slots, parents), F32)
        for f in range(entries):
            total += jnp.where(slot == wanted[f : f + 1, :], table_ref[k, f : f + 1, :], 0.0)
        out_ref[k] = total.T.astype(BF16)


def far_weights(far_sources, far_delays, translation):
    parents, _, band = translation.shape
    return pl.pallas_call(
        weights_kernel,
        out_shape=jax.ShapeDtypeStruct((band, parents, LAGS * parents), BF16),
        compiler_params=params(),
        name="weights",
    )(far_sources.T, far_delays.T, jnp.transpose(translation, (2, 1, 0)))


def translate_kernel(rows, places, weights_ref, *refs):
    inputs, out_ref, wide, result_ref = refs[:-4], refs[-4], refs[-3:-1], refs[-1]
    band, parents, _ = weights_ref.shape
    for source, scratch in zip(inputs, wide):
        scratch[: source.shape[0], :] = source[...].astype(F32)
    result_ref[...] = jnp.zeros_like(result_ref)
    for k in range(band):
        picked = [
            wide[array][pl.ds(start + k, parents, stride=stride), :].astype(BF16)
            for array, start, stride in places
        ]
        total = matmul(weights_ref[k], jnp.concatenate(picked, axis=0))
        result_ref[pl.ds(k, parents, stride=rows), :] = total
    out_ref[...] = result_ref[...].astype(BF16)


def translate(weights, rows, newest, oldest):
    _, parents, _ = weights.shape
    arrays, places = [], []
    for array, start, stride in (newest, oldest):
        known = [i for i, other in enumerate(arrays) if other is array]
        if not known:
            arrays.append(array)
        places.append((known[0] if known else len(arrays) - 1, start, stride))
    columns = newest[0].shape[1]
    longest = max(array.shape[0] for array in arrays)
    return pl.pallas_call(
        functools.partial(translate_kernel, rows, tuple(places)),
        out_shape=jax.ShapeDtypeStruct((parents * rows, columns), BF16),
        scratch_shapes=[
            pltpu.VMEM((longest, columns), F32),
            pltpu.VMEM((longest, columns), F32),
            pltpu.VMEM((parents * rows, columns), F32),
        ],
        compiler_params=params(),
        name="translate",
    )(weights, *arrays)


def near_kernel(step, leads, first_ref, ids_ref, mask_ref, incident_ref, blocks_ref, *refs):
    sources, refs = refs[: 3 * LAGS], refs[3 * LAGS :]
    out_ref, window_ref, matrices_ref, field_ref, sems, block_sems, out_sems = refs
    groups, slots = matrices_ref.shape[:2]
    parts = groups // UNIT
    dead = window_ref.shape[1] - 1

    def load(i):
        chosen = pl.ds(i * UNIT, UNIT)
        return pltpu.make_async_copy(blocks_ref.at[chosen], matrices_ref.at[chosen], block_sems.at[i])

    def save(i):
        chosen = pl.ds(i * UNIT, UNIT)
        return pltpu.make_async_copy(field_ref.at[chosen], out_ref.at[chosen], out_sems.at[i])

    moves = [pltpu.make_async_copy(incident_ref.at[step], field_ref, sems.at[0])]
    for index, lead in enumerate(leads):
        for side in range(3):
            source = sources[index * 3 + side]
            target = window_ref.at[index, pl.ds(side * groups, groups)]
            moves.append(
                pltpu.make_async_copy(
                    source if lead is None else source.at[lead], target, sems.at[index * 3 + side + 1]
                )
            )
    for move in moves:
        move.start()
    for i in range(3):
        load(i).start()
    for index in range(LAGS):
        window_ref[index, dead] = jnp.zeros(window_ref.shape[2:], window_ref.dtype)
    for move in moves:
        move.wait()

    def body(i, carry):
        load(i).wait()

        @pl.when(i + 3 < parts)
        def _():
            load(i + 3).start()

        for j in range(UNIT):
            g = i * UNIT + j
            total = field_ref[g]
            for n in range(slots):
                picked = jnp.where(mask_ref[g, n] != 0, ids_ref[g, n] - first_ref[0], dead)
                for index in range(LAGS):
                    total -= matmul(matrices_ref[g, n, index], window_ref[index, picked])
            field_ref[g] = total
        save(i).start()
        return carry

    lax.fori_loop(0, parts, body, 0)
    for i in range(parts):
        save(i).wait()


def near_field(places, incident, step, near_blocks, windows):
    groups, slots, _, unknowns, _ = near_blocks.shape
    columns = incident.shape[-1]
    arrays = [array for parts, _ in windows for array in parts]
    leads = tuple(lead for _, lead in windows)
    return pl.pallas_call(
        functools.partial(near_kernel, step, leads),
        in_specs=[pl.BlockSpec(memory_space=pltpu.SMEM)] * 3 + [HBM] * (2 + len(arrays)),
        out_specs=HBM,
        out_shape=jax.ShapeDtypeStruct((groups, unknowns, columns), F32),
        scratch_shapes=[
            pltpu.VMEM((LAGS, 3 * groups + 1, unknowns, columns), BF16),
            pltpu.VMEM((groups, slots, LAGS, unknowns, unknowns), BF16),
            pltpu.VMEM((groups, unknowns, columns), F32),
            pltpu.SemaphoreType.DMA((3 * LAGS + 1,)),
            pltpu.SemaphoreType.DMA((groups // UNIT,)),
            pltpu.SemaphoreType.DMA((groups // UNIT,)),
        ],
        compiler_params=params(),
        name="near",
    )(*places, incident, near_blocks, *arrays)


def solve_kernel(step, aliased, *refs):
    last = step == STEPS - 1
    inputs = refs[:6]
    count = 1 if last else 3
    outs = refs[6 + aliased : 6 + aliased + count]
    scratch = refs[6 + aliased + count :]
    buffers, (currents_ref, spectra_ref, in_sems, out_sems) = scratch[:6], scratch[6:]
    loads = [
        pltpu.make_async_copy(source, buffer, in_sems.at[i])
        for i, (source, buffer) in enumerate(zip(inputs, buffers))
        if not (last and i == 5)
    ]
    for load in loads:
        load.start()
    arriving_ref, in_ref, shift_ref, base_ref, inverse_ref, outward_ref = buffers
    children, _, columns = base_ref.shape
    pairs = [(c, c + 1) for c in range(0, children, 2)]
    stores = []

    def store(source, target):
        stores.append(pltpu.make_async_copy(source, target, out_sems.at[len(stores)]))
        stores[-1].start()

    for i in range(3):
        loads[i].wait()
    arriving = arriving_ref[...]
    fields = []
    for pair in pairs:
        received = jnp.concatenate(
            [shift_ref[:, d : d + 1] * arriving for d in pair], axis=1
        )
        fields.append(matmul(in_ref[...], received))
    for i in range(3, 5):
        loads[i].wait()
    for pair, field in zip(pairs, fields):
        for i, d in enumerate(pair):
            drive = (base_ref[d] - field[:, i * columns : (i + 1) * columns]).astype(BF16)
            currents_ref[d] = matmul(inverse_ref[d], drive).astype(BF16)
    store(currents_ref, outs[0].at[step])
    if not last:
        store(currents_ref, outs[1])
        loads[5].wait()
        spectra = None
        for pair in pairs:
            spread = matmul(
                outward_ref[...], jnp.concatenate([currents_ref[d] for d in pair], axis=1)
            )
            for i, d in enumerate(pair):
                term = shift_ref[:, d : d + 1].astype(F32) * spread[:, i * columns : (i + 1) * columns]
                spectra = term if spectra is None else spectra + term
        spectra_ref[...] = spectra.astype(BF16)
        store(spectra_ref, outs[2])
    for copy in stores:
        copy.wait()


def solve(step, results, arriving, base, self_inverse, ray_in, ray_out, shift):
    last = step == STEPS - 1
    groups, unknowns, columns = base.shape
    operands = [arriving, ray_in, shift, base, self_inverse, ray_out]
    buffers = [pltpu.VMEM(a.shape, a.dtype) for a in operands]
    aliased = results is not None
    out_shape = [jax.ShapeDtypeStruct((STEPS, groups, unknowns, columns), BF16)]
    if not last:
        out_shape += [
            jax.ShapeDtypeStruct((groups, unknowns, columns), BF16),
            jax.ShapeDtypeStruct(arriving.shape, BF16),
        ]
    if aliased:
        operands.append(results)
    return pl.pallas_call(
        functools.partial(solve_kernel, step, aliased),
        in_specs=[HBM] * len(operands),
        out_specs=[HBM] * len(out_shape),
        out_shape=out_shape,
        input_output_aliases={len(operands) - 1: 0} if aliased else {},
        scratch_shapes=buffers
        + [
            pltpu.VMEM((groups, unknowns, columns), BF16),
            pltpu.VMEM(arriving.shape, BF16),
            pltpu.SemaphoreType.DMA((6,)),
            pltpu.SemaphoreType.DMA((3,)),
        ],
        compiler_params=params(),
        name="solve",
    )(*operands)


def shifted(block, distance):
    devices = range(lax.axis_size(AXES))
    route = [(i - distance, i) for i in devices if i - distance in devices]
    return lax.ppermute(block, AXES, route)


def window(block):
    return [shifted(block, 1), block, shifted(block, -1)]


def exchange(block, messages):
    tall, columns = block.shape
    cut = block.reshape(messages, tall // messages // 2, 2, columns)
    moved = lax.all_to_all(cut, AXES, split_axis=0, concat_axis=0, tiled=True)
    return moved.reshape(tall, columns)


def on_device(
    incident,
    currents_past,
    spectra_past,
    self_inverse,
    near_blocks,
    neighbours,
    near_mask,
    ray_out,
    ray_in,
    child_shift,
    far_sources,
    far_delays,
    translation,
):
    groups = self_inverse.shape[0]
    messages, band = translation.shape[0], translation.shape[2]
    rows = band + band % 2
    first_group = (lax.axis_index(AXES) - 1) * groups
    places = (first_group.reshape(1), neighbours, near_mask)
    packed = pack(spectra_past[:, 0], band, rows)
    opening = exchange(packed, messages)
    past = window(currents_past)
    bands = [(opening, lag * rows, LAGS * rows) for lag in range(LAGS)]
    windows = [(past, 0), (past, 1)]
    rays = pad_rays(ray_in, ray_out, child_shift, band, rows)
    weights = far_weights(far_sources, far_delays, translation)
    weights, rays = lax.optimization_barrier((weights, rays))
    results = None
    for step in range(STEPS):
        arriving = exchange(translate(weights, rows, *bands), messages)
        base = near_field(places, incident, step, near_blocks, windows)
        results, *rest = solve(step, results, arriving, base, self_inverse, *rays)
        if rest:
            current, spectra = rest
            moved = exchange(spectra, messages)
            nearby = window(current)
            windows = [(nearby, None), windows[0]]
            bands = [(moved, 0, rows), bands[0]]
    return results


def solution(mesh):
    in_specs = (
        P(None, AXES, None, None),
        P(None, AXES, None, None),
        P(None, AXES, None, None),
        P(AXES, None, None),
        P(AXES, None, None, None, None),
        P(AXES, None),
        P(AXES, None),
        P(),
        P(),
        P(),
        P(),
        P(),
        P(None, None, AXES),
    )
    out_specs = P(None, AXES, None, None)
    return jax.shard_map(
        on_device, mesh=mesh, in_specs=in_specs, out_specs=out_specs, check_vma=False
    )
```

```python
import functools

import jax
import jax.numpy as jnp
import numpy as np
from jax import lax
from jax.experimental import pallas as pl
from jax.experimental.pallas import tpu as pltpu
from jax.sharding import PartitionSpec as P

LAGS = 2
STEPS = 4
AXES = ("grp", "dir")
CHUNK = 16
UNIT = 1
PIECES = 4
BF16 = jnp.bfloat16
F32 = jnp.float32
HBM = pl.BlockSpec(memory_space=pltpu.HBM)


def params():
    return pltpu.CompilerParams(vmem_limit_bytes=64 << 20)


def matmul(left, right):
    return jnp.dot(left, right, preferred_element_type=F32)


def spread_matrix(band, rows):
    out = np.zeros((CHUNK * rows, CHUNK * band), np.float32)
    for b in range(CHUNK):
        for i in range(band):
            out[b * rows + i, b * band + i] = 1.0
    return out


def pack_kernel(rows, past_ref, out_ref, taken_ref, wide_ref, result_ref, rounded_ref, in_sems, out_sems):
    lags, directions, columns = past_ref.shape
    parents = out_ref.shape[0] // (lags * rows)
    band = directions // parents
    part = out_ref.shape[0] // PIECES
    loads = [
        pltpu.make_async_copy(past_ref.at[lag], taken_ref.at[lag], in_sems.at[lag]) for lag in range(lags)
    ]
    for load in loads:
        load.start()
    for lag in range(lags):
        for k in range(band, rows):
            result_ref[pl.ds(lag * rows + k, parents, stride=lags * rows), :] = jnp.zeros((parents, columns), F32)
        loads[lag].wait()
        wide_ref[lag] = taken_ref[lag].astype(F32)
        for k in range(band):
            result_ref[pl.ds(lag * rows + k, parents, stride=lags * rows), :] = wide_ref[
                lag, pl.ds(k, parents, stride=band), :
            ]
    stores = []
    for piece in range(PIECES):
        chosen = pl.ds(piece * part, part)
        rounded_ref[chosen, :] = result_ref[chosen, :].astype(BF16)
        stores.append(pltpu.make_async_copy(rounded_ref.at[chosen], out_ref.at[chosen], out_sems.at[piece]))
        stores[-1].start()
    for store in stores:
        store.wait()


def pack(past, band, rows):
    lags, directions, columns = past.shape
    tall = directions // band * lags * rows
    return pl.pallas_call(
        functools.partial(pack_kernel, rows),
        in_specs=[HBM],
        out_specs=HBM,
        out_shape=jax.ShapeDtypeStruct((tall, columns), BF16),
        scratch_shapes=[
            pltpu.VMEM(past.shape, BF16),
            pltpu.VMEM(past.shape, F32),
            pltpu.VMEM((tall, columns), F32),
            pltpu.VMEM((tall, columns), BF16),
            pltpu.SemaphoreType.DMA((lags,)),
            pltpu.SemaphoreType.DMA((PIECES,)),
        ],
        compiler_params=params(),
        name="pack",
    )(past)


def rays_kernel(select_ref, ray_in_ref, ray_out_ref, shift_ref, in_ref, out_ref, shift_out_ref):
    tall, wide = select_ref.shape
    select = select_ref[...]
    outgoing = ray_out_ref[...].astype(F32).T
    shift = shift_ref[...]
    shift = jnp.concatenate([shift, jnp.zeros((128 - shift.shape[0], shift.shape[1]), F32)]).T
    incoming = []
    for m in range(ray_in_ref.shape[0] // wide):
        at, to = m * wide, pl.ds(m * tall, tall)
        incoming.append(matmul(select, ray_in_ref[pl.ds(at, wide), :]))
        out_ref[to, :] = matmul(select, outgoing[at : at + wide, :].astype(BF16)).astype(BF16)
        shift_out_ref[to, :] = matmul(select, shift[at : at + wide, :].astype(BF16)).astype(BF16)
    in_ref[...] = jnp.concatenate(incoming).T.astype(BF16)


def pad_rays(ray_in, ray_out, child_shift, band, rows):
    select = jnp.asarray(spread_matrix(band, rows), BF16)
    padded = ray_in.shape[0] // band * rows
    return pl.pallas_call(
        rays_kernel,
        out_shape=(
            jax.ShapeDtypeStruct((ray_in.shape[1], padded), BF16),
            jax.ShapeDtypeStruct((padded, ray_out.shape[0]), BF16),
            jax.ShapeDtypeStruct((padded, 128), BF16),
        ),
        compiler_params=params(),
        name="rays",
    )(select, ray_in, ray_out, child_shift)


def weights_kernel(sources_ref, delays_ref, table_ref, out_ref):
    band, entries, parents = table_ref.shape
    slots = LAGS * parents
    slot = lax.broadcasted_iota(jnp.int32, (slots, parents), 0)
    wanted = (delays_ref[...] - 1) * parents + sources_ref[...]
    for k in range(band):
        total = jnp.zeros((slots, parents), F32)
        for f in range(entries):
            total += jnp.where(slot == wanted[f : f + 1, :], table_ref[k, f : f + 1, :], 0.0)
        out_ref[k] = total.T.astype(BF16)


def far_weights(far_sources, far_delays, translation):
    parents, _, band = translation.shape
    return pl.pallas_call(
        weights_kernel,
        out_shape=jax.ShapeDtypeStruct((band, parents, LAGS * parents), BF16),
        compiler_params=params(),
        name="weights",
    )(far_sources.T, far_delays.T, jnp.transpose(translation, (2, 1, 0)))


def translate_kernel(rows, places, weights_ref, *refs):
    inputs, out_ref, wide, result_ref = refs[:-4], refs[-4], refs[-3:-1], refs[-1]
    band, parents, _ = weights_ref.shape
    for source, scratch in zip(inputs, wide):
        scratch[: source.shape[0], :] = source[...].astype(F32)
    result_ref[...] = jnp.zeros_like(result_ref)
    for k in range(band):
        picked = [
            wide[array][pl.ds(start + k, parents, stride=stride), :].astype(BF16)
            for array, start, stride in places
        ]
        total = matmul(weights_ref[k], jnp.concatenate(picked, axis=0))
        result_ref[pl.ds(k, parents, stride=rows), :] = total
    out_ref[...] = result_ref[...].astype(BF16)


def translate(weights, rows, newest, oldest):
    _, parents, _ = weights.shape
    arrays, places = [], []
    for array, start, stride in (newest, oldest):
        known = [i for i, other in enumerate(arrays) if other is array]
        if not known:
            arrays.append(array)
        places.append((known[0] if known else len(arrays) - 1, start, stride))
    columns = newest[0].shape[1]
    longest = max(array.shape[0] for array in arrays)
    return pl.pallas_call(
        functools.partial(translate_kernel, rows, tuple(places)),
        out_shape=jax.ShapeDtypeStruct((parents * rows, columns), BF16),
        scratch_shapes=[
            pltpu.VMEM((longest, columns), F32),
            pltpu.VMEM((longest, columns), F32),
            pltpu.VMEM((parents * rows, columns), F32),
        ],
        compiler_params=params(),
        name="translate",
    )(weights, *arrays)


def near_kernel(step, leads, first_ref, ids_ref, mask_ref, incident_ref, blocks_ref, *refs):
    sources, refs = refs[: 3 * LAGS], refs[3 * LAGS :]
    out_ref, window_ref, matrices_ref, field_ref, sems, block_sems, out_sems = refs
    groups, slots = matrices_ref.shape[:2]
    parts = groups // UNIT
    dead = window_ref.shape[1] - 1

    def load(i):
        chosen = pl.ds(i * UNIT, UNIT)
        return pltpu.make_async_copy(blocks_ref.at[chosen], matrices_ref.at[chosen], block_sems.at[i])

    def save(i):
        chosen = pl.ds(i * UNIT, UNIT)
        return pltpu.make_async_copy(field_ref.at[chosen], out_ref.at[chosen], out_sems.at[i])

    moves = [pltpu.make_async_copy(incident_ref.at[step], field_ref, sems.at[0])]
    for index, lead in enumerate(leads):
        for side in range(3):
            source = sources[index * 3 + side]
            target = window_ref.at[index, pl.ds(side * groups, groups)]
            moves.append(
                pltpu.make_async_copy(
                    source if lead is None else source.at[lead], target, sems.at[index * 3 + side + 1]
                )
            )
    for move in moves:
        move.start()
    for i in range(3):
        load(i).start()
    for index in range(LAGS):
        window_ref[index, dead] = jnp.zeros(window_ref.shape[2:], window_ref.dtype)
    for move in moves:
        move.wait()

    def body(i, carry):
        load(i).wait()

        @pl.when(i + 3 < parts)
        def _():
            load(i + 3).start()

        for j in range(UNIT):
            g = i * UNIT + j
            total = field_ref[g]
            for n in range(slots):
                picked = jnp.where(mask_ref[g, n] != 0, ids_ref[g, n] - first_ref[0], dead)
                for index in range(LAGS):
                    total -= matmul(matrices_ref[g, n, index], window_ref[index, picked])
            field_ref[g] = total
        save(i).start()
        return carry

    lax.fori_loop(0, parts, body, 0)
    for i in range(parts):
        save(i).wait()


def near_field(places, incident, step, near_blocks, windows):
    groups, slots, _, unknowns, _ = near_blocks.shape
    columns = incident.shape[-1]
    arrays = [array for parts, _ in windows for array in parts]
    leads = tuple(lead for _, lead in windows)
    return pl.pallas_call(
        functools.partial(near_kernel, step, leads),
        in_specs=[pl.BlockSpec(memory_space=pltpu.SMEM)] * 3 + [HBM] * (2 + len(arrays)),
        out_specs=HBM,
        out_shape=jax.ShapeDtypeStruct((groups, unknowns, columns), F32),
        scratch_shapes=[
            pltpu.VMEM((LAGS, 3 * groups + 1, unknowns, columns), BF16),
            pltpu.VMEM((groups, slots, LAGS, unknowns, unknowns), BF16),
            pltpu.VMEM((groups, unknowns, columns), F32),
            pltpu.SemaphoreType.DMA((3 * LAGS + 1,)),
            pltpu.SemaphoreType.DMA((groups // UNIT,)),
            pltpu.SemaphoreType.DMA((groups // UNIT,)),
        ],
        compiler_params=params(),
        name="near",
    )(*places, incident, near_blocks, *arrays)


def solve_kernel(step, aliased, *refs):
    last = step == STEPS - 1
    inputs = refs[:6]
    count = 1 if last else 3
    outs = refs[6 + aliased : 6 + aliased + count]
    scratch = refs[6 + aliased + count :]
    buffers, (currents_ref, spectra_ref, in_sems, out_sems) = scratch[:6], scratch[6:]
    loads = [
        pltpu.make_async_copy(source, buffer, in_sems.at[i])
        for i, (source, buffer) in enumerate(zip(inputs, buffers))
        if not (last and i == 5)
    ]
    for load in loads:
        load.start()
    arriving_ref, in_ref, shift_ref, base_ref, inverse_ref, outward_ref = buffers
    children, _, columns = base_ref.shape
    pairs = [(c, c + 1) for c in range(0, children, 2)]
    stores = []

    def store(source, target):
        stores.append(pltpu.make_async_copy(source, target, out_sems.at[len(stores)]))
        stores[-1].start()

    for i in range(3):
        loads[i].wait()
    arriving = arriving_ref[...]
    fields = []
    for pair in pairs:
        received = jnp.concatenate(
            [shift_ref[:, d : d + 1] * arriving for d in pair], axis=1
        )
        fields.append(matmul(in_ref[...], received))
    for i in range(3, 5):
        loads[i].wait()
    for pair, field in zip(pairs, fields):
        for i, d in enumerate(pair):
            drive = (base_ref[d] - field[:, i * columns : (i + 1) * columns]).astype(BF16)
            currents_ref[d] = matmul(inverse_ref[d], drive).astype(BF16)
    store(currents_ref, outs[0].at[step])
    if not last:
        store(currents_ref, outs[1])
        loads[5].wait()
        spectra = None
        for pair in pairs:
            spread = matmul(
                outward_ref[...], jnp.concatenate([currents_ref[d] for d in pair], axis=1)
            )
            for i, d in enumerate(pair):
                term = shift_ref[:, d : d + 1].astype(F32) * spread[:, i * columns : (i + 1) * columns]
                spectra = term if spectra is None else spectra + term
        spectra_ref[...] = spectra.astype(BF16)
        store(spectra_ref, outs[2])
    for copy in stores:
        copy.wait()


def solve(step, results, arriving, base, self_inverse, ray_in, ray_out, shift):
    last = step == STEPS - 1
    groups, unknowns, columns = base.shape
    operands = [arriving, ray_in, shift, base, self_inverse, ray_out]
    buffers = [pltpu.VMEM(a.shape, a.dtype) for a in operands]
    aliased = results is not None
    out_shape = [jax.ShapeDtypeStruct((STEPS, groups, unknowns, columns), BF16)]
    if not last:
        out_shape += [
            jax.ShapeDtypeStruct((groups, unknowns, columns), BF16),
            jax.ShapeDtypeStruct(arriving.shape, BF16),
        ]
    if aliased:
        operands.append(results)
    return pl.pallas_call(
        functools.partial(solve_kernel, step, aliased),
        in_specs=[HBM] * len(operands),
        out_specs=[HBM] * len(out_shape),
        out_shape=out_shape,
        input_output_aliases={len(operands) - 1: 0} if aliased else {},
        scratch_shapes=buffers
        + [
            pltpu.VMEM((groups, unknowns, columns), BF16),
            pltpu.VMEM(arriving.shape, BF16),
            pltpu.SemaphoreType.DMA((6,)),
            pltpu.SemaphoreType.DMA((3,)),
        ],
        compiler_params=params(),
        name="solve",
    )(*operands)


def shifted(block, distance):
    devices = range(lax.axis_size(AXES))
    route = [(i - distance, i) for i in devices if i - distance in devices]
    return lax.ppermute(block, AXES, route)


def window(block):
    return [shifted(block, 1), block, shifted(block, -1)]


def exchange(block, messages):
    tall, columns = block.shape
    cut = block.reshape(messages, tall // messages // 2, 2, columns)
    moved = lax.all_to_all(cut, AXES, split_axis=0, concat_axis=0, tiled=True)
    return moved.reshape(tall, columns)


def on_device(
    incident,
    currents_past,
    spectra_past,
    self_inverse,
    near_blocks,
    neighbours,
    near_mask,
    ray_out,
    ray_in,
    child_shift,
    far_sources,
    far_delays,
    translation,
):
    groups = self_inverse.shape[0]
    messages, band = translation.shape[0], translation.shape[2]
    rows = band + band % 2
    first_group = (lax.axis_index(AXES) - 1) * groups
    places = (first_group.reshape(1), neighbours, near_mask)
    packed = pack(spectra_past[:, 0], band, band)
    opening = exchange(packed, messages)
    past = window(currents_past)
    bands = [(opening, lag * band, LAGS * band) for lag in range(LAGS)]
    windows = [(past, 0), (past, 1)]
    rays = pad_rays(ray_in, ray_out, child_shift, band, rows)
    weights = far_weights(far_sources, far_delays, translation)
    weights, rays = lax.optimization_barrier((weights, rays))
    results = None
    for step in range(STEPS):
        arriving = exchange(translate(weights, rows, *bands), messages)
        base = near_field(places, incident, step, near_blocks, windows)
        results, *rest = solve(step, results, arriving, base, self_inverse, *rays)
        if rest:
            current, spectra = rest
            moved = exchange(spectra, messages)
            after = shifted(current, -1)
            nearby = [shifted(current, 1), current, after]
            windows = [(nearby, None), windows[0]]
            bands = [(moved, 0, rows), bands[0]]
    return results


def solution(mesh):
    in_specs = (
        P(None, AXES, None, None),
        P(None, AXES, None, None),
        P(None, AXES, None, None),
        P(AXES, None, None),
        P(AXES, None, None, None, None),
        P(AXES, None),
        P(AXES, None),
        P(),
        P(),
        P(),
        P(),
        P(),
        P(None, None, AXES),
    )
    out_specs = P(None, AXES, None, None)
    return jax.shard_map(
        on_device, mesh=mesh, in_specs=in_specs, out_specs=out_specs, check_vma=False
    )
```
